256 devices in a mesh: rows: 8 (over z), vocab: 32 (over y, x, core).
Axes of the slice: x: 4, y: 4, z: 8, core: 2. Of those that a mesh axis runs over, the one named last changes fastest.
Arguments:
- hidden: bfloat16 [1024, 8192], P('rows', 'vocab'), may hold values from -30 to 30
- head: bfloat16 [8192, 152064], P(None, ('vocab', 'rows')), may hold values from -1 to 1
- states: int32 [1024], replicated, may hold values from 0 to 2047
- class_of: int32 [152064], P('vocab'), may hold values from 0 to 255, as said below
- table: int32 [2048, 8], replicated, may hold values from -2147483648 to 2147483646, as said below
Outputs:
- log_probs: float32 [1024, 152064], P('rows', 'vocab')
- entropy: float32 [1024], P('rows')
The draws below stay inside these ranges and needn't reach their ends.
Inputs may be any that keep to these rules, and one draw needn't show every extreme that they name: `class_of`: class 0 is the class of at least one token. `table`: bit 0 of word 0 is set in every state, so class 0 is allowed everywhere.
All inputs are finite; a program needn't handle non-finite values.
Results may differ from the reference program's by a relative error of at most 0.0003.
Values may be sent and summed in bfloat16 or wider, within the bound.
No kernel may reach another device: no remote copies, remote signals or barrier semaphores. Data moves between devices by JAX's collectives and lax.ppermute only.
A program may use at most 128 MiB of HBM per device.

```python
import jax
import jax.numpy as jnp
from jax import lax

D = 8192
V = 152064
STATES = 2048
CLASSES = 256
ROWS = 1024


def head_block(key, index):
    block_key = jax.random.fold_in(jax.random.fold_in(key, 101), index)
    values = jax.random.normal(block_key, (D, V // 64), jnp.float32) * D ** (-0.5)
    return jnp.clip(values, -1.0, 1.0)


def special_pairs(key):
    base = jax.random.fold_in(key, 103)
    blocks = jax.random.randint(jax.random.fold_in(base, 1), (6,), 0, 64)
    first = jax.random.randint(jax.random.fold_in(base, 2), (6,), 0, V // 64)
    offset = jax.random.randint(jax.random.fold_in(base, 3), (6,), 1, V // 64)
    second = (first + offset) % (V // 64)
    return (blocks, first, second)


def narrow_block(key):

    def build(index):
        return head_block(key, index).astype(jnp.bfloat16)
    return build


def draw_head(key, part):
    blocks = lax.map(narrow_block(key), jnp.arange(64, dtype=jnp.int32))
    return jnp.transpose(blocks, (1, 0, 2)).reshape(D, V).astype(jnp.bfloat16)


def draw_hidden(key, part):
    values = jax.random.normal(jax.random.fold_in(key, 201), (ROWS, D), jnp.float32) * 3.0
    values = jnp.clip(values, -18.0, 18.0)
    return jnp.clip(values, -30.0, 30.0).astype(jnp.bfloat16)


def draw_class_of(key, part):
    classes = jax.random.randint(jax.random.fold_in(key, 301), (V,), 0, CLASSES)
    blocks, first, second = special_pairs(key)
    width = V // 64
    classes = classes.at[blocks * width + first].set(0)
    classes = classes.at[blocks * width + second].set(0)
    return classes.astype(jnp.int32)


def draw_table(key, part):
    words = jax.random.randint(jax.random.fold_in(key, 401), (STATES, CLASSES // 32), -2147483648, 2147483647, jnp.int32)
    return words.at[:, 0].set(jnp.bitwise_or(words[:, 0], 1)).astype(jnp.int32)


def touch_ends(entries, key, smallest, top_value):
    longest = entries.shape.index(max(entries.shape))
    spots = []
    for shift in (0, 1):
        where = [jax.random.randint(jax.random.fold_in(key, axis), (), 0, length) for axis, length in enumerate(entries.shape)]
        where[longest] = (where[longest] + shift) % entries.shape[longest]
        spots.append(tuple(where))
    return entries.at[spots[0]].set(smallest).at[spots[1]].set(top_value)


def setup_inputs(seed: int = 0) -> dict:
    seeds = jax.random.split(jax.random.key(seed), 6)
    hidden = draw_hidden(jax.random.fold_in(seeds[5], 71), 0)
    head = draw_head(jax.random.fold_in(seeds[5], 71), 0)
    states = touch_ends(jax.random.randint(seeds[2], (ROWS,), 0, STATES), jax.random.fold_in(seeds[2], 1), 0, STATES - 1).astype(jnp.int32)
    class_of = draw_class_of(jax.random.fold_in(seeds[5], 71), 0)
    table = draw_table(jax.random.fold_in(seeds[5], 71), 0)
    return {"hidden": hidden, "head": head, "states": states, "class_of": class_of, "table": table}


def reference(hidden, head, states, class_of, table):
    logits = jnp.dot(hidden, head, preferred_element_type=jnp.float32)
    words = jnp.take(table, states, axis=0)
    shifts = jnp.arange(32, dtype=jnp.int32)
    bit_values = jnp.bitwise_and(jnp.right_shift(words[:, :, None], shifts[None, None, :]), 1)
    allowed_class = bit_values.reshape(words.shape[0], words.shape[1] * 32)
    allowed = jnp.take(allowed_class, class_of, axis=1) > 0
    peak = jnp.max(jnp.where(allowed, logits, -1.0e30), axis=1)
    weights = jnp.where(allowed, jnp.exp(logits - peak[:, None]), 0.0)
    total = jnp.sum(weights, axis=1)
    weighted = jnp.sum(weights * logits, axis=1)
    norm_log = peak + jnp.log(total)
    log_probs = jnp.where(allowed, logits - norm_log[:, None], 0.0)
    entropy = norm_log - weighted / total
    return log_probs, entropy
```

```python
import functools

import jax
import jax.numpy as jnp
from jax import lax
from jax.experimental import pallas as pl
from jax.experimental.pallas import tpu as pltpu
from jax.sharding import PartitionSpec as P

masked_floor = -1e30
side = 4
levels = 65520.0
vmem_bytes = 24 * 2**20
padded = 608
far_offsets = (4, 3, -3, 2, -2)
near_offsets = (1, -1, 0)


def plane_shift(lead, step):
    pairs = []
    for y in range(side):
        for x in range(side):
            for core in range(2):
                along_x = (core == 0) == lead
                to_y = y if along_x else (y + step) % side
                to_x = (x + step) % side if along_x else x
                pairs.append(((y * side + x) * 2 + core, (to_y * side + to_x) * 2 + core))
    return pairs


def sent(block, pairs):
    return lax.ppermute(block, "vocab", pairs)


def from_row_group(block, offset):
    count = lax.axis_size("rows")
    return lax.ppermute(block, "rows", [((k + offset) % count, k) for k in range(count)])


def swapped(block):
    count = lax.axis_size("vocab")
    return lax.ppermute(block, "vocab", [(k, k ^ 1) for k in range(count)])


def ring(block, lead):
    half = block.shape[0] // 2
    before = sent(block, plane_shift(lead, 1))
    after = sent(block, plane_shift(lead, -1))
    far_low = sent(before[:half], plane_shift(lead, 1))
    far_high = sent(after[half:], plane_shift(lead, -1))
    return before, after, far_low, far_high


def block_numbers(core):
    place = lax.axis_index("vocab")
    x, y = place // 2 % side, place // (2 * side)
    lead = jnp.where(core == 0, x, y)
    other = jnp.where(core == 0, y, x)
    leads = (0, -1, 1, 2)
    steps = [(a, 0) for a in leads] + [(a, -1) for a in leads] + [(a, 1) for a in leads]
    steps += [(a, 2) for a in leads]
    ahead = (lead + jnp.array([a for a, _ in steps], jnp.int32)) % side
    across = (other + jnp.array([b for _, b in steps], jnp.int32)) % side
    chip = jnp.where(core == 0, across * side + ahead, ahead * side + across)
    return (2 * chip + core).astype(jnp.int32)


def dotted(weight, part):
    return lax.dot_general(
        weight, part, (((1,), (1,)), ((), ())), preferred_element_type=jnp.float32
    )


def encode(logits, width):
    row = lax.broadcasted_iota(jnp.int32, logits.shape, 0)
    real = row < width
    low = jnp.min(jnp.where(real, logits, -masked_floor), axis=0, keepdims=True)
    high = jnp.max(jnp.where(real, logits, masked_floor), axis=0, keepdims=True)
    base = 0.5 * low + 0.5 * high
    span = jnp.maximum(high - low, 1e-30)
    grade = jnp.ceil(jnp.log2(span / levels) * 256.0)
    inverse = jnp.exp2(grade * (-1.0 / 256.0))
    codes = jnp.clip(jnp.round((logits - base) * inverse), -32767.0, 32767.0)
    size = jnp.ceil(jnp.log2(jnp.maximum(jnp.abs(base), 1e-30) / 32767.0))
    unit = jnp.exp2(size)
    first = jnp.clip(jnp.round(base / unit), -32767.0, 32767.0)
    second = jnp.clip(jnp.round((base - first * unit) / unit * 32767.0), -32767.0, 32767.0)
    for at, value in enumerate((grade, size, first, second)):
        codes = jnp.where(row == width + at, value, codes)
    return codes.astype(jnp.int32).astype(jnp.int16)


def logits_body(numbers, *refs, parts, keep):
    pieces, weights, outs, total = refs[:parts], refs[parts], refs[parts + 1 : -1], refs[-1]
    width, depth = weights.shape[0], pieces[0].shape[2]
    total[width:, :] = jnp.zeros((total.shape[0] - width, total.shape[1]), jnp.float32)
    acc, at = None, 0
    for piece in pieces:
        for k in range(piece.shape[0]):
            start = pl.multiple_of(numbers[at] * depth, depth)
            term = dotted(weights[:, pl.ds(start, depth)], piece[k])
            acc = term if acc is None else acc + term
            at += 1
    total[:width, :] = acc
    for k, out in enumerate(outs):
        logits = total[:, k * 128 : (k + 1) * 128]
        out[...] = logits if k == keep else encode(logits, width)


def group_logits(pieces, weights_t, numbers, keep):
    count = pieces[0].shape[1]
    width = weights_t.shape[0]
    outs = [
        jax.ShapeDtypeStruct((padded, 128), jnp.float32 if k == keep else jnp.int16)
        for k in range(count // 128)
    ]
    return pl.pallas_call(
        functools.partial(logits_body, parts=len(pieces), keep=keep),
        out_shape=outs,
        in_specs=[pl.BlockSpec(memory_space=pltpu.SMEM)]
        + [pl.BlockSpec(memory_space=pltpu.VMEM)] * (len(pieces) + 1),
        scratch_shapes=[pltpu.VMEM((padded, count), jnp.float32)],
        compiler_params=pltpu.CompilerParams(vmem_limit_bytes=vmem_bytes),
        cost_estimate=pl.CostEstimate(
            flops=2 * count * weights_t.size, transcendentals=0, bytes_accessed=weights_t.size * 2
        ),
        name="group_logits",
    )(numbers, *pieces, weights_t)


def decode_body(place, mask, own, *refs, offsets):
    codes, out, stats, held = refs[:-3], *refs[-3:]
    groups, width, count = held.shape
    here = place[0]
    held[here] = own[:width, :]
    for offset, code in zip(offsets, codes):
        values = code[...].astype(jnp.int32).astype(jnp.float32)
        grade, size = values[width : width + 1], values[width + 1 : width + 2]
        first, second = values[width + 2 : width + 3], values[width + 3 : width + 4]
        base = (first + second * (1.0 / 32767.0)) * jnp.exp2(size)
        step = jnp.exp2(grade * (1.0 / 256.0))
        held[(here - offset) % groups] = values[:width] * step + base
    top = jnp.full((1, count), masked_floor, jnp.float32)
    for k in range(groups):
        span = slice(k * width, (k + 1) * width)
        logits = jnp.where(mask[span, :] > 0.5, held[k], masked_floor)
        out[span, :] = logits
        top = jnp.maximum(top, jnp.max(logits, axis=0, keepdims=True))
    logits = out[...]
    weights = jnp.where(logits > 0.5 * masked_floor, jnp.exp(logits - top), 0.0)
    stats[0:1, :] = top
    stats[1:2, :] = jnp.sum(weights, axis=0, keepdims=True)
    stats[2:3, :] = jnp.sum(weights * logits, axis=0, keepdims=True)


def decoded(mask, own, codes, offsets, width):
    groups = lax.axis_size("rows")
    count = own.shape[1]
    place = lax.axis_index("rows").astype(jnp.int32).reshape(1)
    return pl.pallas_call(
        functools.partial(decode_body, offsets=offsets),
        out_shape=(
            jax.ShapeDtypeStruct((groups * width, count), jnp.float32),
            jax.ShapeDtypeStruct((3, count), jnp.float32),
        ),
        in_specs=[pl.BlockSpec(memory_space=pltpu.SMEM)]
        + [pl.BlockSpec(memory_space=pltpu.VMEM)] * (2 + len(codes)),
        scratch_shapes=[pltpu.VMEM((groups, width, count), jnp.float32)],
        compiler_params=pltpu.CompilerParams(vmem_limit_bytes=vmem_bytes),
        name="decode",
    )(place, mask, own, *codes)


def mask_body(states, table, classes, out):
    entries, count = table.shape[1], states.shape[1]
    chosen = lax.broadcasted_iota(jnp.int32, (entries, count), 0) == states[...]
    chosen = chosen.astype(jnp.float32).astype(jnp.bfloat16)
    words = table[...]
    found = []
    for at in range(4):
        piece = jnp.bitwise_and(jnp.right_shift(words, 8 * at), 255)
        piece = piece.astype(jnp.float32).astype(jnp.bfloat16)
        found.append(jnp.dot(piece, chosen, preferred_element_type=jnp.float32).astype(jnp.int32))
    pieces = jnp.stack(found, axis=1)[:, :, None, :]
    shifts = lax.broadcasted_iota(jnp.int32, (1, 1, 8, 1), 2)
    bits = jnp.bitwise_and(jnp.right_shift(pieces, shifts), 1).reshape(words.shape[0] * 32, count)
    allowed = bits.astype(jnp.float32).astype(jnp.bfloat16)
    total = out.shape[0]
    for at in range(0, total, 128):
        size = min(128, total - at)
        spread = lax.broadcasted_iota(jnp.int32, (allowed.shape[0], 128), 0) == classes[:, at : at + 128]
        spread = spread.astype(jnp.float32).astype(jnp.bfloat16)
        piece = lax.dot_general(
            spread, allowed, (((0,), (0,)), ((), ())), preferred_element_type=jnp.float32
        )
        out[at : at + size, :] = piece[:size]


def token_mask(states, table, class_of):
    total = class_of.shape[0]
    classes = jnp.pad(class_of, (0, -total % 128)).reshape(1, -1)
    return pl.pallas_call(
        mask_body,
        out_shape=jax.ShapeDtypeStruct((total, states.shape[0]), jnp.float32),
        compiler_params=pltpu.CompilerParams(vmem_limit_bytes=vmem_bytes),
        name="mask",
    )(states.reshape(1, -1), table.T, classes)


def merged(shard):
    count = lax.axis_size("vocab")
    copies = jnp.broadcast_to(shard, (count, *shard.shape))
    every = lax.all_to_all(copies, "vocab", split_axis=0, concat_axis=0, tiled=True)
    top = jnp.max(every[:, 0], axis=0)
    scale = jnp.exp(every[:, 0] - top)
    return top, jnp.sum(every[:, 1] * scale, axis=0), jnp.sum(every[:, 2] * scale, axis=0)


def on_device(hidden, head, states, class_of, table):
    count, depth = hidden.shape
    width = head.shape[1]
    core = lax.axis_index("vocab") % 2
    numbers = jnp.concatenate((block_numbers(core), block_numbers(1 - core)))

    found = {0: hidden, 1: from_row_group(hidden, 1), -1: from_row_group(hidden, -1)}
    above = from_row_group(jnp.concatenate((found[0], found[1]), axis=0), 2)
    below = from_row_group(jnp.concatenate((found[0], found[-1]), axis=0), -2)
    found[2], found[3] = above[:count], above[count:]
    found[-2], found[-3] = below[:count], below[count:]
    found[4] = from_row_group(hidden, 4)

    near = jnp.concatenate([found[s] for s in near_offsets], axis=0)
    near_line = jnp.concatenate((near, *ring(near, True)), axis=0)
    far = jnp.concatenate([found[s] for s in far_offsets], axis=0)
    far_line = jnp.concatenate((far, *ring(far, True)), axis=0)

    head_t = head.T
    own_states = lax.dynamic_slice_in_dim(states, lax.axis_index("rows") * count, count, 0)
    mask = token_mask(own_states, table, class_of)

    codes, offsets, own = [], [], None
    for offset_list, line in ((far_offsets, far_line), (near_offsets, near_line)):
        mine = (line, *ring(line, False))
        both = (*mine, *(swapped(part) for part in mine))
        size = len(offset_list) * count
        both = [part.reshape(-1, size, depth) for part in both]
        keep = offset_list.index(0) if 0 in offset_list else None
        for s, piece in zip(offset_list, group_logits(both, head_t, numbers, keep)):
            if s == 0:
                own = piece
            else:
                codes.append(from_row_group(piece, -s))
                offsets.append(s)

    logits, stats = decoded(mask, own, codes, tuple(offsets), width)
    peak, total, weighted = merged(stats)
    norm_log = peak + jnp.log(total)
    log_probs = jnp.where(logits > 0.5 * masked_floor, logits - norm_log[None, :], 0.0)
    return log_probs.T, norm_log - weighted / total


def solution(mesh):
    in_specs = (P("rows", "vocab"), P(None, ("vocab", "rows")), P(), P("vocab"), P())
    out_specs = (P("rows", "vocab"), P("rows"))
    return jax.shard_map(
        on_device, mesh=mesh, in_specs=in_specs, out_specs=out_specs, check_vma=False
    )
```

```python
import functools

import jax
import jax.numpy as jnp
from jax import lax
from jax.experimental import pallas as pl
from jax.experimental.pallas import tpu as pltpu
from jax.sharding import PartitionSpec as P

masked_floor = -1e30
side = 4
levels = 65520.0
vmem_bytes = 24 * 2**20
padded = 608
far_offsets = (4, 3, -3, 2)
near_offsets = (-2, -1, 1, 0)


def plane_shift(lead, step):
    pairs = []
    for y in range(side):
        for x in range(side):
            for core in range(2):
                along_x = (core == 0) == lead
                to_y = y if along_x else (y + step) % side
                to_x = (x + step) % side if along_x else x
                pairs.append(((y * side + x) * 2 + core, (to_y * side + to_x) * 2 + core))
    return pairs


def sent(block, pairs):
    return lax.ppermute(block, "vocab", pairs)


def from_row_group(block, offset):
    count = lax.axis_size("rows")
    return lax.ppermute(block, "rows", [((k + offset) % count, k) for k in range(count)])


def swapped(block):
    count = lax.axis_size("vocab")
    return lax.ppermute(block, "vocab", [(k, k ^ 1) for k in range(count)])


def tied(value, other):
    return value if other is None else lax.optimization_barrier((value, other))[0]


def ring_ends(block, lead):
    return sent(block, plane_shift(lead, 1)), sent(block, plane_shift(lead, -1))


def ring_far(before, after, lead, gate=None):
    half = before.shape[0] // 2
    low, high = tied(before[:half], gate), tied(after[half:], gate)
    return sent(low, plane_shift(lead, 1)), sent(high, plane_shift(lead, -1))


def block_numbers(core):
    place = lax.axis_index("vocab")
    x, y = place // 2 % side, place // (2 * side)
    lead = jnp.where(core == 0, x, y)
    other = jnp.where(core == 0, y, x)
    leads = (0, -1, 1, 2)
    steps = [(a, 0) for a in leads] + [(a, -1) for a in leads] + [(a, 1) for a in leads]
    steps += [(a, 2) for a in leads]
    ahead = (lead + jnp.array([a for a, _ in steps], jnp.int32)) % side
    across = (other + jnp.array([b for _, b in steps], jnp.int32)) % side
    chip = jnp.where(core == 0, across * side + ahead, ahead * side + across)
    return jnp.append(chip, core).astype(jnp.int32)


def encode(logits, width):
    row = lax.broadcasted_iota(jnp.int32, logits.shape, 0)
    real = row < width
    low = jnp.min(jnp.where(real, logits, -masked_floor), axis=0, keepdims=True)
    high = jnp.max(jnp.where(real, logits, masked_floor), axis=0, keepdims=True)
    base = 0.5 * low + 0.5 * high
    span = jnp.maximum(high - low, 1e-30)
    grade = jnp.ceil(jnp.log2(span / levels) * 256.0)
    inverse = jnp.exp2(grade * (-1.0 / 256.0))
    codes = jnp.clip(jnp.round((logits - base) * inverse), -32767.0, 32767.0)
    size = jnp.ceil(jnp.log2(jnp.maximum(jnp.abs(base), 1e-30) / 32767.0))
    unit = jnp.exp2(size)
    first = jnp.clip(jnp.round(base / unit), -32767.0, 32767.0)
    second = jnp.clip(jnp.round((base - first * unit) / unit * 32767.0), -32767.0, 32767.0)
    for at, value in enumerate((grade, size, first, second)):
        codes = jnp.where(row == width + at, value, codes)
    return codes.astype(jnp.int32).astype(jnp.int16)


def logits_body(numbers, *refs, keep):
    mine, theirs, head, outs = refs[:5], refs[5:10], refs[10], refs[11:-4]
    buffer, weights, total, arrived = refs[-4:]
    width, depth = head.shape[0], mine[0].shape[1]
    count = total.shape[1]
    own_rows = pl.ds(pl.multiple_of(numbers[16] * depth, depth), depth)
    other_rows = pl.ds(pl.multiple_of((1 - numbers[16]) * depth, depth), depth)

    def fetch(at, across, ahead):
        first = mine[across].at[ahead] if across < 3 else mine[3 + ahead // 2].at[ahead % 2]
        second = theirs[ahead].at[across] if ahead < 3 else theirs[3 + across // 2].at[across % 2]
        lanes = pl.ds(pl.multiple_of(numbers[at] * 2 * depth, 2 * depth), 2 * depth)
        return (
            pltpu.make_async_copy(head.at[:, lanes], weights.at[at], arrived.at[at, 0]),
            pltpu.make_async_copy(first, buffer.at[at, own_rows, :], arrived.at[at, 1]),
            pltpu.make_async_copy(second, buffer.at[at, other_rows, :], arrived.at[at, 2]),
        )

    for at in range(16):
        for copy in fetch(at, at // 4, at % 4):
            copy.start()
    total[...] = jnp.zeros(total.shape, jnp.float32)

    def one(at, carry):
        for copy in fetch(at, 0, 0):
            copy.wait()
        total[:width, :] += jnp.dot(weights[at], buffer[at], preferred_element_type=jnp.float32)
        return carry

    lax.fori_loop(0, 16, one, 0)
    for k, out in enumerate(outs):
        logits = total[:, k * 128 : (k + 1) * 128]
        out[...] = logits if k == keep else encode(logits, width)


def group_logits(mine, theirs, head_t, numbers, keep):
    depth, count = mine[0].shape[1:]
    outs = [
        jax.ShapeDtypeStruct((padded, 128), jnp.float32 if k == keep else jnp.int16)
        for k in range(count // 128)
    ]
    return pl.pallas_call(
        functools.partial(logits_body, keep=keep),
        out_shape=outs,
        in_specs=[pl.BlockSpec(memory_space=pltpu.SMEM)] + [pl.BlockSpec(memory_space=pltpu.HBM)] * 11,
        scratch_shapes=[
            pltpu.VMEM((16, 2 * depth, count), jnp.bfloat16),
            pltpu.VMEM((16, head_t.shape[0], 2 * depth), jnp.bfloat16),
            pltpu.VMEM((padded, count), jnp.float32),
            pltpu.SemaphoreType.DMA((16, 3)),
        ],
        compiler_params=pltpu.CompilerParams(vmem_limit_bytes=56 * 2**20),
        cost_estimate=pl.CostEstimate(
            flops=2 * count * head_t.size, transcendentals=0, bytes_accessed=head_t.size * 2
        ),
        name="group_logits",
    )(numbers, *mine, *theirs, head_t)


def order_body(*refs):
    out, width = refs[-1], refs[0].shape[1]
    half = (len(refs) - 1) // 2
    for k, block in enumerate(refs[:-1]):
        out[k // half, :, (k % half) * width : (k % half + 1) * width] = block[...]


def ordered(blocks):
    depth, width = blocks[0].shape
    return pl.pallas_call(
        order_body,
        out_shape=jax.ShapeDtypeStruct((2, depth, len(blocks) // 2 * width), blocks[0].dtype),
        compiler_params=pltpu.CompilerParams(vmem_limit_bytes=vmem_bytes),
        name="ordered",
    )(*blocks)


def line_body(own, before, after, low, high, *outs):
    for k, (out, last) in enumerate(zip(outs, (low, high))):
        out[0] = own[k]
        out[1] = before[k]
        out[2] = after[k]
        out[3] = last[0]


def lines(own, *parts):
    return pl.pallas_call(
        line_body,
        out_shape=[jax.ShapeDtypeStruct((4, *own.shape[1:]), own.dtype)] * 2,
        compiler_params=pltpu.CompilerParams(vmem_limit_bytes=vmem_bytes),
        name="lines",
    )(own, *parts)


def decode_body(place, mask, own, *refs, offsets):
    codes, out, stats, held = refs[:-3], *refs[-3:]
    groups, width, count = held.shape
    here = place[0]
    held[here] = own[:width, :]
    for offset, code in zip(offsets, codes):
        values = code[...].astype(jnp.int32).astype(jnp.float32)
        grade, size = values[width : width + 1], values[width + 1 : width + 2]
        first, second = values[width + 2 : width + 3], values[width + 3 : width + 4]
        base = (first + second * (1.0 / 32767.0)) * jnp.exp2(size)
        step = jnp.exp2(grade * (1.0 / 256.0))
        held[(here - offset) % groups] = values[:width] * step + base
    top = jnp.full((1, count), masked_floor, jnp.float32)
    for k in range(groups):
        span = slice(k * width, (k + 1) * width)
        logits = jnp.where(mask[span, :] > 0.5, held[k], masked_floor)
        out[span, :] = logits
        top = jnp.maximum(top, jnp.max(logits, axis=0, keepdims=True))
    logits = out[...]
    weights = jnp.where(logits > 0.5 * masked_floor, jnp.exp(logits - top), 0.0)
    stats[0:1, :] = top
    stats[1:2, :] = jnp.sum(weights, axis=0, keepdims=True)
    stats[2:3, :] = jnp.sum(weights * logits, axis=0, keepdims=True)


def decoded(mask, own, codes, offsets, width):
    groups = lax.axis_size("rows")
    count = own.shape[1]
    place = lax.axis_index("rows").astype(jnp.int32).reshape(1)
    return pl.pallas_call(
        functools.partial(decode_body, offsets=offsets),
        out_shape=(
            jax.ShapeDtypeStruct((groups * width, count), jnp.float32),
            jax.ShapeDtypeStruct((3, count), jnp.float32),
        ),
        in_specs=[pl.BlockSpec(memory_space=pltpu.SMEM)]
        + [pl.BlockSpec(memory_space=pltpu.VMEM)] * (2 + len(codes)),
        scratch_shapes=[pltpu.VMEM((groups, width, count), jnp.float32)],
        compiler_params=pltpu.CompilerParams(vmem_limit_bytes=vmem_bytes),
        name="decode",
    )(place, mask, own, *codes)


def mask_body(states, table, classes, out):
    entries, count = table.shape[1], states.shape[1]
    chosen = lax.broadcasted_iota(jnp.int32, (entries, count), 0) == states[...]
    chosen = chosen.astype(jnp.float32).astype(jnp.bfloat16)
    words = table[...]
    found = []
    for at in range(4):
        piece = jnp.bitwise_and(jnp.right_shift(words, 8 * at), 255)
        piece = piece.astype(jnp.float32).astype(jnp.bfloat16)
        found.append(jnp.dot(piece, chosen, preferred_element_type=jnp.float32).astype(jnp.int32))
    pieces = jnp.stack(found, axis=1)[:, :, None, :]
    shifts = lax.broadcasted_iota(jnp.int32, (1, 1, 8, 1), 2)
    bits = jnp.bitwise_and(jnp.right_shift(pieces, shifts), 1).reshape(words.shape[0] * 32, count)
    allowed = bits.astype(jnp.float32).astype(jnp.bfloat16)
    total = out.shape[0]
    for at in range(0, total, 128):
        size = min(128, total - at)
        spread = lax.broadcasted_iota(jnp.int32, (allowed.shape[0], 128), 0) == classes[:, at : at + 128]
        spread = spread.astype(jnp.float32).astype(jnp.bfloat16)
        piece = lax.dot_general(
            spread, allowed, (((0,), (0,)), ((), ())), preferred_element_type=jnp.float32
        )
        out[at : at + size, :] = piece[:size]


def token_mask(states, table, class_of):
    total = class_of.shape[0]
    classes = jnp.pad(class_of, (0, -total % 128)).reshape(1, -1)
    return pl.pallas_call(
        mask_body,
        out_shape=jax.ShapeDtypeStruct((total, states.shape[0]), jnp.float32),
        compiler_params=pltpu.CompilerParams(vmem_limit_bytes=vmem_bytes),
        name="mask",
    )(states.reshape(1, -1), table.T, classes)


def merged(shard):
    count = lax.axis_size("vocab")
    copies = jnp.broadcast_to(shard, (count, *shard.shape))
    every = lax.all_to_all(copies, "vocab", split_axis=0, concat_axis=0, tiled=True)
    top = jnp.max(every[:, 0], axis=0)
    scale = jnp.exp(every[:, 0] - top)
    return top, jnp.sum(every[:, 1] * scale, axis=0), jnp.sum(every[:, 2] * scale, axis=0)


def on_device(hidden, head, states, class_of, table):
    count, depth = hidden.shape
    width = head.shape[1]
    core = lax.axis_index("vocab") % 2
    numbers = block_numbers(core)
    hidden_t = hidden.T
    found = [hidden_t if s == 0 else from_row_group(hidden_t, s) for s in (*far_offsets, *near_offsets)]
    block = ordered(found)
    ends = ring_ends(block, True)
    far_line, near_line = lines(block, *ends, *ring_far(*ends, True))

    head_t = head.T
    own_states = lax.dynamic_slice_in_dim(states, lax.axis_index("rows") * count, count, 0)
    mask = token_mask(own_states, table, class_of)

    codes, offsets, own = [], [], None
    behind, made = None, None
    for offset_list, line in ((far_offsets, far_line), (near_offsets, near_line)):
        line = tied(line, behind)
        ends = ring_ends(line, False)
        mine = [line, *ends, *ring_far(*ends, False, made)]
        behind = (mine[3], mine[4])
        theirs = [swapped(part) for part in mine]
        keep = offset_list.index(0) if 0 in offset_list else None
        pieces = group_logits(mine, theirs, head_t, numbers, keep)
        made = pieces[0]
        for s, piece in zip(offset_list, pieces):
            if s == 0:
                own = piece
            else:
                codes.append(from_row_group(piece, -s))
                offsets.append(s)

    logits, stats = decoded(mask, own, codes, tuple(offsets), width)
    peak, total, weighted = merged(stats)
    norm_log = peak + jnp.log(total)
    log_probs = jnp.where(logits > 0.5 * masked_floor, logits - norm_log[None, :], 0.0)
    return log_probs.T, norm_log - weighted / total


def solution(mesh):
    in_specs = (P("rows", "vocab"), P(None, ("vocab", "rows")), P(), P("vocab"), P())
    out_specs = (P("rows", "vocab"), P("rows"))
    return jax.shard_map(
        on_device, mesh=mesh, in_specs=in_specs, out_specs=out_specs, check_vma=False
    )
```

```python
import functools

import jax
import jax.numpy as jnp
from jax import lax
from jax.experimental import pallas as pl
from jax.experimental.pallas import tpu as pltpu
from jax.sharding import PartitionSpec as P

masked_floor = -1e30
side = 4
levels = 65520.0
vmem_bytes = 24 * 2**20
padded = 608
far_offsets = (4, 3, -3, 2)
near_offsets = (-2, -1, 1, 0)


def plane_shift(lead, step):
    pairs = []
    for y in range(side):
        for x in range(side):
            for core in range(2):
                along_x = (core == 0) == lead
                to_y = y if along_x else (y + step) % side
                to_x = (x + step) % side if along_x else x
                pairs.append(((y * side + x) * 2 + core, (to_y * side + to_x) * 2 + core))
    return pairs


def sent(block, pairs):
    return lax.ppermute(block, "vocab", pairs)


def from_row_group(block, offset):
    count = lax.axis_size("rows")
    return lax.ppermute(block, "rows", [((k + offset) % count, k) for k in range(count)])


def swapped(block):
    count = lax.axis_size("vocab")
    return lax.ppermute(block, "vocab", [(k, k ^ 1) for k in range(count)])


def tied(value, other):
    return value if other is None else lax.optimization_barrier((value, other))[0]


def ring_ends(block, lead):
    return sent(block, plane_shift(lead, 1)), sent(block, plane_shift(lead, -1))


def ring_far(before, after, lead, gate=None):
    half = before.shape[0] // 2
    low, high = tied(before[:half], gate), tied(after[half:], gate)
    return sent(low, plane_shift(lead, 1)), sent(high, plane_shift(lead, -1))


def block_numbers(core):
    place = lax.axis_index("vocab")
    x, y = place // 2 % side, place // (2 * side)
    lead = jnp.where(core == 0, x, y)
    other = jnp.where(core == 0, y, x)
    leads = (0, -1, 1, 2)
    steps = [(a, 0) for a in leads] + [(a, -1) for a in leads] + [(a, 1) for a in leads]
    steps += [(a, 2) for a in leads]
    ahead = (lead + jnp.array([a for a, _ in steps], jnp.int32)) % side
    across = (other + jnp.array([b for _, b in steps], jnp.int32)) % side
    chip = jnp.where(core == 0, across * side + ahead, ahead * side + across)
    return jnp.append(chip, core).astype(jnp.int32)


def encode(logits, width):
    row = lax.broadcasted_iota(jnp.int32, logits.shape, 0)
    real = row < width
    low = jnp.min(jnp.where(real, logits, -masked_floor), axis=0, keepdims=True)
    high = jnp.max(jnp.where(real, logits, masked_floor), axis=0, keepdims=True)
    base = 0.5 * low + 0.5 * high
    span = jnp.maximum(high - low, 1e-30)
    grade = jnp.ceil(jnp.log2(span / levels) * 256.0)
    inverse = jnp.exp2(grade * (-1.0 / 256.0))
    codes = jnp.clip(jnp.round((logits - base) * inverse), -32767.0, 32767.0)
    size = jnp.ceil(jnp.log2(jnp.maximum(jnp.abs(base), 1e-30) / 32767.0))
    unit = jnp.exp2(size)
    first = jnp.clip(jnp.round(base / unit), -32767.0, 32767.0)
    second = jnp.clip(jnp.round((base - first * unit) / unit * 32767.0), -32767.0, 32767.0)
    for at, value in enumerate((grade, size, first, second)):
        codes = jnp.where(row == width + at, value, codes)
    return codes.astype(jnp.int32).astype(jnp.int16)


def logits_body(numbers, *refs, keep):
    mine, theirs, head, outs = refs[:5], refs[5:10], refs[10], refs[11:-4]
    buffer, weights, total, arrived = refs[-4:]
    width, depth = head.shape[0], mine[0].shape[1]
    count = total.shape[1]
    own_rows = pl.ds(pl.multiple_of(numbers[16] * depth, depth), depth)
    other_rows = pl.ds(pl.multiple_of((1 - numbers[16]) * depth, depth), depth)

    def fetch(at, across, ahead):
        first = mine[across].at[ahead] if across < 3 else mine[3 + ahead // 2].at[ahead % 2]
        second = theirs[ahead].at[across] if ahead < 3 else theirs[3 + across // 2].at[across % 2]
        lanes = pl.ds(pl.multiple_of(numbers[at] * 2 * depth, 2 * depth), 2 * depth)
        return (
            pltpu.make_async_copy(head.at[:, lanes], weights.at[at], arrived.at[at, 0]),
            pltpu.make_async_copy(first, buffer.at[at, own_rows, :], arrived.at[at, 1]),
            pltpu.make_async_copy(second, buffer.at[at, other_rows, :], arrived.at[at, 2]),
        )

    for at in range(16):
        for copy in fetch(at, at // 4, at % 4):
            copy.start()
    total[...] = jnp.zeros(total.shape, jnp.float32)

    def one(at, carry):
        for copy in fetch(at, 0, 0):
            copy.wait()
        total[:width, :] += jnp.dot(weights[at], buffer[at], preferred_element_type=jnp.float32)
        return carry

    lax.fori_loop(0, 16, one, 0)
    for k, out in enumerate(outs):
        logits = total[:, k * 128 : (k + 1) * 128]
        out[...] = logits if k == keep else encode(logits, width)


def group_logits(mine, theirs, head_t, numbers, keep):
    depth, count = mine[0].shape[1:]
    outs = [
        jax.ShapeDtypeStruct((padded, 128), jnp.float32 if k == keep else jnp.int16)
        for k in range(count // 128)
    ]
    return pl.pallas_call(
        functools.partial(logits_body, keep=keep),
        out_shape=outs,
        in_specs=[pl.BlockSpec(memory_space=pltpu.SMEM)] + [pl.BlockSpec(memory_space=pltpu.HBM)] * 11,
        scratch_shapes=[
            pltpu.VMEM((16, 2 * depth, count), jnp.bfloat16),
            pltpu.VMEM((16, head_t.shape[0], 2 * depth), jnp.bfloat16),
            pltpu.VMEM((padded, count), jnp.float32),
            pltpu.SemaphoreType.DMA((16, 3)),
        ],
        compiler_params=pltpu.CompilerParams(vmem_limit_bytes=56 * 2**20),
        cost_estimate=pl.CostEstimate(
            flops=2 * count * head_t.size, transcendentals=0, bytes_accessed=head_t.size * 2
        ),
        name="group_logits",
    )(numbers, *mine, *theirs, head_t)


def order_body(*refs):
    out, width = refs[-1], refs[0].shape[1]
    half = (len(refs) - 1) // 2
    for k, block in enumerate(refs[:-1]):
        out[k // half, :, (k % half) * width : (k % half + 1) * width] = block[...]


def ordered(blocks):
    depth, width = blocks[0].shape
    return pl.pallas_call(
        order_body,
        out_shape=jax.ShapeDtypeStruct((2, depth, len(blocks) // 2 * width), blocks[0].dtype),
        compiler_params=pltpu.CompilerParams(vmem_limit_bytes=vmem_bytes),
        name="ordered",
    )(*blocks)


def line_body(*refs):
    parts, outs = refs[:4], refs[4:]
    for k, out in enumerate(outs):
        for at, part in enumerate(parts):
            out[at] = part[k]


def lines(*parts):
    return pl.pallas_call(
        line_body,
        out_shape=[jax.ShapeDtypeStruct((4, *parts[0].shape[1:]), parts[0].dtype)] * 2,
        compiler_params=pltpu.CompilerParams(vmem_limit_bytes=vmem_bytes),
        name="lines",
    )(*parts)


def decode_body(place, mask, own, *refs, offsets):
    codes, out, stats, held = refs[:-3], *refs[-3:]
    groups, width, count = held.shape
    here = place[0]
    held[here] = own[:width, :]
    for offset, code in zip(offsets, codes):
        values = code[...].astype(jnp.int32).astype(jnp.float32)
        grade, size = values[width : width + 1], values[width + 1 : width + 2]
        first, second = values[width + 2 : width + 3], values[width + 3 : width + 4]
        base = (first + second * (1.0 / 32767.0)) * jnp.exp2(size)
        step = jnp.exp2(grade * (1.0 / 256.0))
        held[(here - offset) % groups] = values[:width] * step + base
    top = jnp.full((1, count), masked_floor, jnp.float32)
    for k in range(groups):
        span = slice(k * width, (k + 1) * width)
        logits = jnp.where(mask[span, :] > 0.5, held[k], masked_floor)
        out[span, :] = logits
        top = jnp.maximum(top, jnp.max(logits, axis=0, keepdims=True))
    logits = out[...]
    weights = jnp.where(logits > 0.5 * masked_floor, jnp.exp(logits - top), 0.0)
    stats[0:1, :] = top
    stats[1:2, :] = jnp.sum(weights, axis=0, keepdims=True)
    stats[2:3, :] = jnp.sum(weights * logits, axis=0, keepdims=True)


def decoded(mask, own, codes, offsets, width):
    groups = lax.axis_size("rows")
    count = own.shape[1]
    place = lax.axis_index("rows").astype(jnp.int32).reshape(1)
    return pl.pallas_call(
        functools.partial(decode_body, offsets=offsets),
        out_shape=(
            jax.ShapeDtypeStruct((groups * width, count), jnp.float32),
            jax.ShapeDtypeStruct((3, count), jnp.float32),
        ),
        in_specs=[pl.BlockSpec(memory_space=pltpu.SMEM)]
        + [pl.BlockSpec(memory_space=pltpu.VMEM)] * (2 + len(codes)),
        scratch_shapes=[pltpu.VMEM((groups, width, count), jnp.float32)],
        compiler_params=pltpu.CompilerParams(vmem_limit_bytes=vmem_bytes),
        name="decode",
    )(place, mask, own, *codes)


def mask_body(states, table, classes, out):
    entries, count = table.shape[1], states.shape[1]
    chosen = lax.broadcasted_iota(jnp.int32, (entries, count), 0) == states[...]
    chosen = chosen.astype(jnp.float32).astype(jnp.bfloat16)
    words = table[...]
    found = []
    for at in range(4):
        piece = jnp.bitwise_and(jnp.right_shift(words, 8 * at), 255)
        piece = piece.astype(jnp.float32).astype(jnp.bfloat16)
        found.append(jnp.dot(piece, chosen, preferred_element_type=jnp.float32).astype(jnp.int32))
    pieces = jnp.stack(found, axis=1)[:, :, None, :]
    shifts = lax.broadcasted_iota(jnp.int32, (1, 1, 8, 1), 2)
    bits = jnp.bitwise_and(jnp.right_shift(pieces, shifts), 1).reshape(words.shape[0] * 32, count)
    allowed = bits.astype(jnp.float32).astype(jnp.bfloat16)
    total = out.shape[0]
    for at in range(0, total, 128):
        size = min(128, total - at)
        spread = lax.broadcasted_iota(jnp.int32, (allowed.shape[0], 128), 0) == classes[:, at : at + 128]
        spread = spread.astype(jnp.float32).astype(jnp.bfloat16)
        piece = lax.dot_general(
            spread, allowed, (((0,), (0,)), ((), ())), preferred_element_type=jnp.float32
        )
        out[at : at + size, :] = piece[:size]


def token_mask(states, table, class_of):
    total = class_of.shape[0]
    classes = jnp.pad(class_of, (0, -total % 128)).reshape(1, -1)
    return pl.pallas_call(
        mask_body,
        out_shape=jax.ShapeDtypeStruct((total, states.shape[0]), jnp.float32),
        compiler_params=pltpu.CompilerParams(vmem_limit_bytes=vmem_bytes),
        name="mask",
    )(states.reshape(1, -1), table.T, classes)


def merged(shard):
    count = lax.axis_size("vocab")
    copies = jnp.broadcast_to(shard, (count, *shard.shape))
    every = lax.all_to_all(copies, "vocab", split_axis=0, concat_axis=0, tiled=True)
    top = jnp.max(every[:, 0], axis=0)
    scale = jnp.exp(every[:, 0] - top)
    return top, jnp.sum(every[:, 1] * scale, axis=0), jnp.sum(every[:, 2] * scale, axis=0)


def on_device(hidden, head, states, class_of, table):
    count, depth = hidden.shape
    width = head.shape[1]
    core = lax.axis_index("vocab") % 2
    numbers = block_numbers(core)
    hidden_t = hidden.T
    found = [hidden_t if s == 0 else from_row_group(hidden_t, s) for s in (*far_offsets, *near_offsets)]
    block = ordered(found)
    opposite = sent(block, plane_shift(True, 2))
    far_line, near_line = lines(block, *ring_ends(block, True), opposite)

    head_t = head.T
    own_states = lax.dynamic_slice_in_dim(states, lax.axis_index("rows") * count, count, 0)
    mask = token_mask(own_states, table, class_of)

    codes, offsets, own = [], [], None
    behind, made = None, None
    for offset_list, line in ((far_offsets, far_line), (near_offsets, near_line)):
        line = tied(line, behind)
        ends = ring_ends(line, False)
        mine = [line, *ends, *ring_far(*ends, False, made)]
        behind = (mine[3], mine[4])
        theirs = [swapped(part) for part in mine]
        keep = offset_list.index(0) if 0 in offset_list else None
        pieces = group_logits(mine, theirs, head_t, numbers, keep)
        made = pieces[0]
        for s, piece in zip(offset_list, pieces):
            if s == 0:
                own = piece
            else:
                codes.append(from_row_group(piece, -s))
                offsets.append(s)

    logits, stats = decoded(mask, own, codes, tuple(offsets), width)
    peak, total, weighted = merged(stats)
    norm_log = peak + jnp.log(total)
    log_probs = jnp.where(logits > 0.5 * masked_floor, logits - norm_log[None, :], 0.0)
    return log_probs.T, norm_log - weighted / total


def solution(mesh):
    in_specs = (P("rows", "vocab"), P(None, ("vocab", "rows")), P(), P("vocab"), P())
    out_specs = (P("rows", "vocab"), P("rows"))
    return jax.shard_map(
        on_device, mesh=mesh, in_specs=in_specs, out_specs=out_specs, check_vma=False
    )
```
